32 devices in a mesh: rep: 1, ep: 32 (over z, y, x, core).
Axes of the slice: x: 2, y: 2, z: 4, core: 2. Of those that a mesh axis runs over, the one named last changes fastest.
Arguments:
- tokens: bfloat16 [512, 3584], P(('rep', 'ep')), may hold values from -6 to 6
- routes: int32 [512, 8], P(('rep', 'ep')), may hold values from 0 to 15, all different within a row; in each aligned block of 16 rows (0 to 15, 16 to 31, ...) at most 16 rows name the same one
- gate_weights: float32 [512, 8], P(('rep', 'ep')), may hold values from 0.05 to 0.5
- w_gate: bfloat16 [32, 3584, 512], P('ep'), may hold values from -0.09375 to 0.09375
- w_up: bfloat16 [32, 3584, 512], P('ep'), may hold values from -0.09375 to 0.09375
- w_down: bfloat16 [32, 512, 3584], P('ep'), may hold values from -0.1875 to 0.1875
Outputs:
- mixed: bfloat16 [512, 3584], P(('rep', 'ep'))
The draws below stay inside these ranges and needn't reach their ends.
Inputs may be any that keep to these rules, and one draw needn't show every extreme that they name: `routes`: each token names 8 different experts. Among the tokens of one device at most 16 name any one expert, and in every draw some expert is named by exactly 16 tokens of some device.
All inputs are finite; a program needn't handle non-finite values.
Results may differ from the reference program's by a relative error of at most 0.008.
Values may be sent and summed in bfloat16 or wider, within the bound.
No kernel may reach another device: no remote copies, remote signals or barrier semaphores. Data moves between devices by JAX's collectives and lax.ppermute only.
A program may use at most 128 MiB of HBM per device.

```python
import math
import jax
import jax.numpy as jnp
import numpy as np
from jax import lax

D = 3584
FF = 1024
TOP = 8
TOK_DEV = 16
EXPERTS = 16
CAP = 16
TOKENS = 512
N_EP = 32


def steps_of(stream_key, extent, pieces, smallest, largest):
    gain, own = 1.0, jax.random.fold_in(stream_key, 6)
    for dim, shards_of in pieces:
        draws = jnp.exp(jax.random.uniform(jax.random.fold_in(own, dim), (shards_of,), jnp.float32, smallest / len(pieces), largest / len(pieces)))
        gain = gain * jnp.repeat(draws, extent[dim] // shards_of).reshape([-1 if axis == dim else 1 for axis in range(len(extent))])
    return gain


def assign_block(stream_key, own, number, rows, count, top, limit, lean):
    order = jax.random.permutation(stream_key, count)
    packed, usual = shares(count, rows * top, limit, lean, True), shares(count, rows * top, limit, lean, False)
    places = jnp.arange(count)

    def named(tallies, rotation):
        used = int((tallies > 0).sum())
        fixed = max(1, used // 4)
        moved = fixed + (places - fixed + rotation * (used - fixed)) % max(1, count - fixed)
        return jnp.zeros((count,), jnp.int32).at[order[jnp.where(places < fixed, places, moved)]].set(jnp.asarray(tallies, jnp.int32))

    tallies = jnp.where(number % 4 == 0, named(packed, number // 4), named(usual, number - number // 4 - 1))
    mixed = jax.random.permutation(jax.random.fold_in(own, 3), count)
    giver, sink = mixed[0:count // 2 * 2:2], mixed[1:count // 2 * 2:2]
    margin = jnp.minimum(tallies[giver] - 1, limit - tallies[sink]) // 2
    margin = jnp.where((giver == order[0]) | (sink == order[0]) | (tallies[sink] == 0), 0, jnp.maximum(margin, 0))
    moved = jax.random.randint(jax.random.fold_in(own, 4), (count // 2,), 0, 1 << 20) % (margin + 1)
    tallies = tallies.at[giver].add(-moved).at[sink].add(moved)
    items = jnp.searchsorted(jnp.cumsum(tallies), jnp.arange(rows * top), side="right").astype(jnp.int32)
    listing = items.reshape(top, rows).T
    listing = listing[jax.random.permutation(jax.random.fold_in(own, 1), rows)]
    rotation = jax.random.randint(jax.random.fold_in(own, 2), (rows, 1), 0, top)
    return jnp.take_along_axis(listing, (jnp.arange(top)[None, :] + rotation) % top, axis=1)


def shares(number_of, total, limit, skew, full):
    weights = [(1 << 20) // math.isqrt(standing ** skew) + 1 for standing in range(1, number_of + 1)]
    largest = limit if full else min(limit, max(-(-total // number_of), total * weights[0] // sum(weights)))
    least = 1 if total - largest >= number_of - 1 else 0
    holding, surplus = [largest] + [least] * (number_of - 1), total - largest - least * (number_of - 1)
    while surplus > 0:
        free = [i for i in range(1, number_of) if holding[i] < largest] or [i for i in range(1, number_of) if holding[i] < limit]
        whole, remaining = sum([weights[i] for i in free]), surplus
        for i in free:
            more = min(limit - holding[i], max(1, remaining * weights[i] // whole), surplus)
            holding[i] = holding[i] + more
            surplus = surplus - more
    return np.array(holding)


def gaussian(rng, extent, scale, bound, cuts=(), kind=jnp.bfloat16):
    gain = steps_of(rng, extent, cuts, -0.22, 0.18) if cuts else 1.0
    values = jax.random.normal(rng, extent, jnp.float32) * scale * gain
    return jnp.minimum(jnp.maximum(values, -bound), bound).astype(kind)


def setup_inputs(seed: int = 0, part: int = 0) -> dict:
    keys = jax.random.split(jax.random.key(seed), 7)
    own_keys = jax.random.split(jax.random.fold_in(keys[6], part), 7)
    tokens = gaussian(own_keys[0], (TOKENS, D), 1.0, 6.0, ((0, 32),))
    routes_keys = jax.random.split(jax.random.fold_in(own_keys[1], 1), TOKENS // TOK_DEV)
    routes_turns = jax.random.permutation(jax.random.fold_in(own_keys[1], 3), TOKENS // TOK_DEV)
    routes = jax.vmap(lambda own, number: assign_block(jax.random.fold_in(own_keys[1], 2), own, number, TOK_DEV, EXPERTS, TOP, CAP, 2))(routes_keys, routes_turns).reshape((TOKENS, TOP))
    gate_weights = jnp.clip(0.05 + 0.45 * jax.random.uniform(own_keys[2], (TOKENS, TOP), jnp.float32) ** steps_of(own_keys[2], (TOKENS, TOP), ((0, 32),), -0.2, 0.2), 0.05, 0.5)
    w_gate = gaussian(keys[3], (2 * EXPERTS, D, FF // 2), D ** -0.5, 0.09375, ((0, 32),))
    w_up = gaussian(keys[4], (2 * EXPERTS, D, FF // 2), D ** -0.5, 0.09375, ((0, 32),))
    w_down = gaussian(keys[5], (2 * EXPERTS, FF // 2, D), FF ** -0.5, 0.1875, ((0, 32),))
    return {"tokens": tokens, "routes": routes, "gate_weights": gate_weights, "w_gate": w_gate, "w_up": w_up, "w_down": w_down}


def slot_positions(chosen, expert_count):
    chosen_hits = jnp.sum((chosen[:, :, None] == jnp.arange(expert_count, dtype=jnp.int32)[None, None, :]).astype(jnp.int32), axis=1, dtype=jnp.int32)
    before = (jnp.cumsum(chosen_hits, axis=0, dtype=jnp.int32) - chosen_hits).astype(jnp.int32)
    return jnp.take_along_axis(before, chosen, axis=1).astype(jnp.int32)


def reference(tokens, routes, gate_weights, w_gate, w_up, w_down):
    block_tokens = tokens.reshape(N_EP, TOK_DEV, D)
    block_routes = routes.reshape(N_EP, TOK_DEV, TOP).astype(jnp.int32)

    def fill_block(token_rows, chosen):
        slot_index = slot_positions(chosen, EXPERTS)
        flat_index = (chosen * CAP + slot_index).reshape(-1).astype(jnp.int32)
        buffer = jnp.zeros((EXPERTS * CAP, D), tokens.dtype).at[flat_index].set(jnp.repeat(token_rows, TOP, axis=0))
        return buffer.reshape(EXPERTS, CAP, D), flat_index

    buffers, flat_all = jax.vmap(fill_block)(block_tokens, block_routes)
    gate_halves = w_gate.reshape(EXPERTS, 2, D, FF // 2)
    up_halves = w_up.reshape(EXPERTS, 2, D, FF // 2)
    down_halves = w_down.reshape(EXPERTS, 2, FF // 2, D)

    def run_expert(expert_index):
        expert_rows = buffers[:, expert_index].reshape(N_EP * CAP, D)
        summed = jnp.zeros((N_EP * CAP, D), jnp.float32)
        for half_index in range(2):
            gate_value = jnp.dot(expert_rows, gate_halves[expert_index, half_index], preferred_element_type=jnp.float32)
            up_value = jnp.dot(expert_rows, up_halves[expert_index, half_index], preferred_element_type=jnp.float32)
            hidden = (jax.nn.silu(gate_value) * up_value).astype(jnp.bfloat16)
            partial_value = jnp.dot(hidden, down_halves[expert_index, half_index], preferred_element_type=jnp.float32).astype(jnp.bfloat16)
            summed = summed + partial_value.astype(jnp.float32)
        return summed.astype(jnp.bfloat16).reshape(N_EP, CAP, D)

    results = lax.map(run_expert, jnp.arange(EXPERTS, dtype=jnp.int32))
    per_source = jnp.swapaxes(results, 0, 1).reshape(N_EP, EXPERTS * CAP, D)

    def gather_back(table, flat_index, weights):
        picked = table[flat_index].reshape(TOK_DEV, TOP, D).astype(jnp.float32)
        return jnp.einsum('tk,tkd->td', weights.astype(jnp.float32), picked)

    mixed = jax.vmap(gather_back)(per_source, flat_all, gate_weights.reshape(N_EP, TOK_DEV, TOP))
    return mixed.reshape(TOKENS, D).astype(jnp.bfloat16)
```

```python
import jax
import jax.numpy as jnp
from jax import lax
from jax.sharding import PartitionSpec as P


def dense_gates(routes, gate_weights, expert_count):
    hits = routes[:, :, None] == jnp.arange(expert_count, dtype=jnp.int32)[None, None, :]
    return jnp.sum(jnp.where(hits, gate_weights[:, :, None], 0.0), axis=1)


def body(tokens, routes, gate_weights, w_gate, w_up, w_down):
    devices = lax.axis_size("ep")
    expert = lax.axis_index("ep") // 2
    gates = dense_gates(routes, gate_weights, devices // 2)
    all_gates = lax.all_gather(gates, "ep", axis=0, tiled=True)
    rows = lax.all_gather(tokens, "ep", axis=0, tiled=True)
    gate_value = jnp.dot(rows, w_gate[0], preferred_element_type=jnp.float32)
    up_value = jnp.dot(rows, w_up[0], preferred_element_type=jnp.float32)
    hidden = (jax.nn.silu(gate_value) * up_value).astype(jnp.bfloat16)
    partial_value = jnp.dot(hidden, w_down[0], preferred_element_type=jnp.float32)
    mine = jnp.arange(devices // 2, dtype=jnp.int32) == expert
    weight = jnp.sum(jnp.where(mine[None, :], all_gates, 0.0), axis=1)
    weighted = (partial_value * weight[:, None]).astype(jnp.bfloat16)
    return lax.psum_scatter(weighted, "ep", scatter_dimension=0, tiled=True)


def solution(mesh):
    placed = (
        P(("rep", "ep"), None),
        P(("rep", "ep"), None),
        P(("rep", "ep"), None),
        P("ep", None, None),
        P("ep", None, None),
        P("ep", None, None),
    )
    return jax.shard_map(
        body, mesh=mesh, in_specs=placed, out_specs=P(("rep", "ep"), None), check_vma=False
    )
```

```python
import jax
import jax.numpy as jnp
from jax import lax
from jax.sharding import PartitionSpec as P


def exchange(value, mask):
    pairs = [(source, source ^ mask) for source in range(lax.axis_size("ep"))]
    return lax.ppermute(value, "ep", pairs)


def tree_plan(bits):
    steps = []
    for hops in range(1, bits):
        chosen = {bit: [] for bit in range(bits)}
        for mask in range(1 << bits):
            if mask.bit_count() == hops:
                held = [bit for bit in range(bits) if mask >> bit & 1]
                bit = min(held, key=lambda candidate: len(chosen[candidate]))
                chosen[bit].append(mask)
        steps.append([(bit, masks) for bit, masks in chosen.items() if masks])
    return steps


def joined(parts):
    return parts[0] if len(parts) == 1 else jnp.concatenate(parts, axis=0)


def gather_rows(own, bits):
    count = own.shape[0]
    held = {0: jnp.concatenate([own, exchange(own, 2 << bits)], axis=0)}
    for step in tree_plan(bits):
        for bit, masks in step:
            arrived = exchange(joined([held[mask ^ (1 << bit)] for mask in masks]), 2 << bit)
            for place, mask in enumerate(masks):
                held[mask] = arrived[2 * count * place : 2 * count * (place + 1)]
    last = (1 << bits) - 1
    halves = [
        exchange(held[last ^ (1 << bit)][bit * count : (bit + 1) * count], 2 << bit)
        for bit in range(2)
    ]
    held[last] = jnp.concatenate(halves, axis=0)
    return held


def added(left, right):
    return (left.astype(jnp.float32) + right.astype(jnp.float32)).astype(left.dtype)


def reduce_rows(held, bits):
    last = (1 << bits) - 1
    count = held[last].shape[0] // 2
    extra = {}
    for bit in range(2):
        rows = slice(bit * count, (bit + 1) * count)
        arrived = exchange(held[last][rows], 2 << bit)
        mask = last ^ (1 << bit)
        halves = [held[mask][:count], held[mask][count:]]
        halves[bit] = added(halves[bit], arrived)
        extra[mask] = jnp.concatenate(halves, axis=0)
    held = {**held, **extra}
    for step in reversed(tree_plan(bits)):
        for bit, masks in step:
            arrived = exchange(joined([held[mask] for mask in masks]), 2 << bit)
            for place, mask in enumerate(masks):
                target = mask ^ (1 << bit)
                piece = arrived[2 * count * place : 2 * count * (place + 1)]
                held[target] = added(held[target], piece)
    arrived = exchange(held[0][count:], 2 << bits)
    return added(held[0][:count], arrived)


def gate_columns(routes, gate_weights, expert_count):
    hits = routes[:, :, None] == jnp.arange(expert_count, dtype=jnp.int32)[None, None, :]
    left = jnp.sum(jnp.where(hits, gate_weights[:, :, None], 0.0), axis=1)
    pieces = []
    for _ in range(3):
        piece = lax.reduce_precision(left, 8, 7)
        pieces.append(piece.astype(jnp.bfloat16))
        left = left - piece
    columns = jnp.concatenate(pieces, axis=1)
    return jnp.pad(columns, ((0, 0), (0, -columns.shape[1] % 128)))


def own_gate(columns, expert, expert_count):
    place = jnp.arange(columns.shape[1], dtype=jnp.int32)
    mine = (place % expert_count == expert) & (place < 3 * expert_count)
    return jnp.sum(jnp.where(mine[None, :], columns.astype(jnp.float32), 0.0), axis=1)[:, None]


def hidden_units(rows, w_gate, w_up):
    gate_value = jnp.dot(rows, w_gate, preferred_element_type=jnp.float32)
    up_value = jnp.dot(rows, w_up, preferred_element_type=jnp.float32)
    return (jax.nn.silu(gate_value) * up_value).astype(jnp.bfloat16)


def body(tokens, routes, gate_weights, w_gate, w_up, w_down):
    devices = lax.axis_size("ep")
    expert_count = devices // 2
    bits = expert_count.bit_length() - 2
    width = tokens.shape[1]
    expert = lax.axis_index("ep") // 2
    columns = gate_columns(routes, gate_weights, expert_count)
    held = gather_rows(jnp.concatenate([tokens, columns], axis=1), bits)
    order = sorted(held, key=lambda mask: mask.bit_count())
    own = jnp.concatenate([held[mask] for mask in order], axis=0)
    other = exchange(own, 1)
    partials = []
    for rows in (other, own):
        hidden = hidden_units(rows[:, :width], w_gate[0], w_up[0])
        value = jnp.dot(hidden, w_down[0], preferred_element_type=jnp.float32)
        partials.append(value * own_gate(rows[:, width:], expert, expert_count))
    arrived = exchange(partials[0].astype(jnp.bfloat16), 1)
    summed = (partials[1] + arrived.astype(jnp.float32)).astype(jnp.bfloat16)
    block = 2 * tokens.shape[0]
    sums = {mask: summed[block * place : block * (place + 1)] for place, mask in enumerate(order)}
    return reduce_rows(sums, bits)


def solution(mesh):
    placed = (
        P(("rep", "ep"), None),
        P(("rep", "ep"), None),
        P(("rep", "ep"), None),
        P("ep", None, None),
        P("ep", None, None),
        P("ep", None, None),
    )
    return jax.shard_map(
        body, mesh=mesh, in_specs=placed, out_specs=P(("rep", "ep"), None), check_vma=False
    )
```

```python
import functools

import jax
import jax.numpy as jnp
from jax import lax
from jax.experimental import pallas as pl
from jax.experimental.pallas import tpu as pltpu
from jax.sharding import PartitionSpec as P


VMEM_MIB = 32


def exchange(value, mask):
    pairs = [(source, source ^ mask) for source in range(lax.axis_size("ep"))]
    return lax.ppermute(value, "ep", pairs)


def tree_plan(bits):
    steps = []
    for hops in range(1, bits):
        chosen = {bit: [] for bit in range(bits)}
        for mask in range(1 << bits):
            if mask.bit_count() == hops:
                held = [bit for bit in range(bits) if mask >> bit & 1]
                bit = min(held, key=lambda candidate: len(chosen[candidate]))
                chosen[bit].append(mask)
        steps.append([(bit, masks) for bit, masks in chosen.items() if masks])
    return steps


def joined(parts):
    return parts[0] if len(parts) == 1 else jnp.concatenate(parts, axis=0)


def gather_rows(tokens, columns, bits):
    count = tokens.shape[0]
    with jax.named_scope("far"):
        far_tokens = exchange(tokens, 2 << bits)
    far_columns = exchange(columns, 2 << bits)
    near = jnp.concatenate([tokens, columns], axis=1)
    far = jnp.concatenate([far_tokens, far_columns], axis=1)
    held = {0: jnp.concatenate([near, far], axis=0)}
    for step in tree_plan(bits):
        for bit, masks in step:
            arrived = exchange(joined([held[mask ^ (1 << bit)] for mask in masks]), 2 << bit)
            for place, mask in enumerate(masks):
                held[mask] = arrived[2 * count * place : 2 * count * (place + 1)]
        masks = [mask for _, group in step for mask in group]
        held.update(zip(masks, lax.optimization_barrier([held[mask] for mask in masks])))
    last = (1 << bits) - 1
    halves = [
        exchange(held[last ^ (1 << bit)][bit * count : (bit + 1) * count], 2 << bit)
        for bit in range(2)
    ]
    held[last] = jnp.concatenate(halves, axis=0)
    return held


def added(left, right):
    return (left.astype(jnp.float32) + right.astype(jnp.float32)).astype(left.dtype)


def reduce_rows(held, bits):
    last = (1 << bits) - 1
    count = held[last].shape[0] // 2
    extra = {}
    for bit in range(2):
        rows = slice(bit * count, (bit + 1) * count)
        arrived = exchange(held[last][rows], 2 << bit)
        mask = last ^ (1 << bit)
        halves = [held[mask][:count], held[mask][count:]]
        halves[bit] = added(halves[bit], arrived)
        extra[mask] = jnp.concatenate(halves, axis=0)
    held = {**held, **extra}
    for step in reversed(tree_plan(bits)):
        for bit, masks in step:
            arrived = exchange(joined([held[mask] for mask in masks]), 2 << bit)
            for place, mask in enumerate(masks):
                target = mask ^ (1 << bit)
                piece = arrived[2 * count * place : 2 * count * (place + 1)]
                held[target] = added(held[target], piece)
    arrived = exchange(held[0][count:], 2 << bits)
    return added(held[0][:count], arrived)


def gate_columns(routes, gate_weights, expert_count):
    hits = routes[:, :, None] == jnp.arange(expert_count, dtype=jnp.int32)[None, None, :]
    left = jnp.sum(jnp.where(hits, gate_weights[:, :, None], 0.0), axis=1)
    pieces = []
    for _ in range(3):
        piece = lax.reduce_precision(left, 8, 7)
        pieces.append(piece.astype(jnp.bfloat16))
        left = left - piece
    columns = jnp.concatenate(pieces, axis=1)
    return jnp.pad(columns, ((0, 0), (0, -columns.shape[1] % 128)))


def expert_kernel(pieces, expert_count, width, chunk, splits, flight, expert_ref, *refs):
    piece_refs, source_refs = refs[:pieces], refs[pieces : pieces + 6]
    out_refs = refs[pieces + 6 : 2 * pieces + 6]
    weight_refs, (rows, hidden, sems) = refs[2 * pieces + 6 : 2 * pieces + 12], refs[2 * pieces + 12 :]
    count = piece_refs[0].shape[0]
    units = weight_refs[0].shape[1]
    depth = width // splits
    jobs = [
        (3 * half + kind, pl.ds(part * depth, depth))
        for half in range(2)
        for part in range(splits)
        for kind in range(2)
    ]
    jobs += [(2, pl.ds(0, units)), (5, pl.ds(0, units))]
    copies = [
        pltpu.make_async_copy(
            source_refs[which].at[part], weight_refs[which].at[part], sems.at[place]
        )
        for place, (which, part) in enumerate(jobs)
    ]
    for copy in copies[:flight]:
        copy.start()
    done = 0
    scales = []
    for place, piece_ref in enumerate(piece_refs):
        rows[place * count : (place + 1) * count, :] = piece_ref[:, :width]
        columns = piece_ref[:, width:].astype(jnp.float32)
        lane = lax.broadcasted_iota(jnp.int32, columns.shape, 1)
        mine = (lax.rem(lane, expert_count) == expert_ref[0]) & (lane < 3 * expert_count)
        scales.append(jnp.sum(jnp.where(mine, columns, 0.0), axis=1, keepdims=True))
    for half in range(2):
        totals = [0.0, 0.0]
        for part in range(splits):
            inner = slice(part * depth, (part + 1) * depth)
            for kind in range(2):
                copies[done].wait()
                if done + flight < len(copies):
                    copies[done + flight].start()
                done += 1
                weight = weight_refs[3 * half + kind][inner, :]
                totals[kind] += jnp.dot(
                    rows[:, inner], weight, preferred_element_type=jnp.float32
                )
        hidden[half] = (jax.nn.silu(totals[0]) * totals[1]).astype(jnp.bfloat16)
    for copy in copies[done:]:
        copy.wait()
    for start in range(0, width, chunk):
        cols = slice(start, start + chunk)
        value = jnp.dot(hidden[0], weight_refs[2][:, cols], preferred_element_type=jnp.float32)
        value += jnp.dot(hidden[1], weight_refs[5][:, cols], preferred_element_type=jnp.float32)
        for place, out_ref in enumerate(out_refs):
            piece = value[place * count : (place + 1) * count] * scales[place]
            out_ref[:, cols] = piece.astype(jnp.bfloat16)


def run_expert(expert, pieces, weights, expert_count):
    count = pieces[0].shape[0]
    units, width = weights[2].shape
    vmem, hbm = pl.BlockSpec(memory_space=pltpu.VMEM), pl.BlockSpec(memory_space=pltpu.HBM)
    rows = count * len(pieces)
    chunk, splits, flight = 512, 2, 3
    weights = [pltpu.with_memory_space_constraint(value, pltpu.HBM) for value in weights]
    return pl.pallas_call(
        functools.partial(expert_kernel, len(pieces), expert_count, width, chunk, splits, flight),
        out_shape=[jax.ShapeDtypeStruct((count, width), jnp.bfloat16)] * len(pieces),
        in_specs=[pl.BlockSpec(memory_space=pltpu.SMEM)] + [vmem] * len(pieces) + [hbm] * 6,
        out_specs=[vmem] * len(pieces),
        scratch_shapes=[pltpu.VMEM(value.shape, value.dtype) for value in weights]
        + [
            pltpu.VMEM((rows, width), jnp.bfloat16),
            pltpu.VMEM((2, rows, units), jnp.bfloat16),
            pltpu.SemaphoreType.DMA((4 * splits + 2,)),
        ],
        cost_estimate=pl.CostEstimate(
            flops=12 * rows * width * units,
            bytes_accessed=12 * width * units + 4 * rows * width,
            transcendentals=2 * rows * units,
        ),
        compiler_params=pltpu.CompilerParams(vmem_limit_bytes=VMEM_MIB * 1024 * 1024),
    )(jnp.reshape(expert, (1,)), *pieces, *weights)


def body(tokens, routes, gate_weights, w_gate, w_up, w_down):
    devices = lax.axis_size("ep")
    expert_count = devices // 2
    bits = expert_count.bit_length() - 2
    expert = lax.axis_index("ep") // 2
    weights = (w_gate[0], w_up[0], w_down[0])
    swapped = tuple(exchange(value, 1) for value in weights)
    columns = gate_columns(routes, gate_weights, expert_count)
    held = gather_rows(tokens, columns, bits)
    order = sorted(held, key=lambda mask: mask.bit_count())
    sums = run_expert(expert, [held[mask] for mask in order], weights + swapped, expert_count)
    return reduce_rows(dict(zip(order, sums)), bits)


def solution(mesh):
    placed = (
        P(("rep", "ep"), None),
        P(("rep", "ep"), None),
        P(("rep", "ep"), None),
        P("ep", None, None),
        P("ep", None, None),
        P("ep", None, None),
    )
    return jax.shard_map(
        body, mesh=mesh, in_specs=placed, out_specs=P(("rep", "ep"), None), check_vma=False
    )
```

```python
import functools

import jax
import jax.numpy as jnp
from jax import lax
from jax.experimental import pallas as pl
from jax.experimental.pallas import tpu as pltpu
from jax.sharding import PartitionSpec as P


RESIDENT, VMEM_MIB = 3, 20


def exchange(value, mask):
    pairs = [(source, source ^ mask) for source in range(lax.axis_size("ep"))]
    return lax.ppermute(value, "ep", pairs)


def tree_plan(bits):
    steps = []
    for hops in range(1, bits):
        chosen = {bit: [] for bit in range(bits)}
        for mask in range(1 << bits):
            if mask.bit_count() == hops:
                held = [bit for bit in range(bits) if mask >> bit & 1]
                bit = min(held, key=lambda candidate: len(chosen[candidate]))
                chosen[bit].append(mask)
        steps.append([(bit, masks) for bit, masks in chosen.items() if masks])
    return steps


def joined(parts):
    return parts[0] if len(parts) == 1 else jnp.concatenate(parts, axis=0)


def gather_tree(own, bits, last_bit):
    count = own.shape[0]
    held = {0: own}
    for step in tree_plan(bits):
        for bit, masks in step:
            arrived = exchange(joined([held[mask ^ (1 << bit)] for mask in masks]), 2 << bit)
            for place, mask in enumerate(masks):
                held[mask] = arrived[count * place : count * (place + 1)]
        masks = [mask for _, group in step for mask in group]
        held.update(zip(masks, lax.optimization_barrier([held[mask] for mask in masks])))
    last = (1 << bits) - 1
    held[last] = exchange(held[last ^ (1 << last_bit)], 2 << last_bit)
    return held


def gather_rows(tokens, columns, bits):
    far_tokens = exchange(tokens, 2 << bits)
    far_columns = exchange(columns, 2 << bits)
    near = gather_tree(jnp.concatenate([tokens, columns], axis=1), bits, 0)
    far = gather_tree(jnp.concatenate([far_tokens, far_columns], axis=1), bits, 1)
    return {mask: (near[mask], far[mask]) for mask in near}


def summed(parts):
    if len(parts) == 1:
        return parts[0]
    total = parts[0].astype(jnp.float32)
    for part in parts[1:]:
        total = total + part.astype(jnp.float32)
    return total.astype(parts[0].dtype)


def added(left, right):
    return summed([left, right])


def reduce_rows(held, bits):
    last = (1 << bits) - 1
    count = held[last].shape[0] // 2
    extra = {}
    for bit in range(2):
        rows = slice(bit * count, (bit + 1) * count)
        arrived = exchange(held[last][rows], 2 << bit)
        mask = last ^ (1 << bit)
        halves = [held[mask][:count], held[mask][count:]]
        halves[bit] = added(halves[bit], arrived)
        extra[mask] = jnp.concatenate(halves, axis=0)
    held = {**held, **extra}
    extra = {}
    steps = tree_plan(bits)
    for step in reversed(steps[1:]):
        for bit, masks in step:
            arrived = exchange(joined([held[mask] for mask in masks]), 2 << bit)
            for place, mask in enumerate(masks):
                piece = arrived[2 * count * place : 2 * count * (place + 1)]
                target = mask ^ (1 << bit)
                if target.bit_count() > 1:
                    held[target] = added(held[target], piece)
                else:
                    extra.setdefault(target, []).append(piece)

    def last_sum(rows):
        parts = [held[0][rows]]
        for bit in range(bits):
            sent = [held[1 << bit][rows]] + [piece[rows] for piece in extra.get(1 << bit, [])]
            parts.append(exchange(summed(sent), 2 << bit))
        return parts

    far = summed(last_sum(slice(count, None)))
    arrived = exchange(far, 2 << bits)
    return summed(last_sum(slice(0, count)) + [arrived])


def gate_columns(routes, gate_weights, expert_count):
    hits = routes[:, :, None] == jnp.arange(expert_count, dtype=jnp.int32)[None, None, :]
    left = jnp.sum(jnp.where(hits, gate_weights[:, :, None], 0.0), axis=1)
    pieces = []
    for _ in range(3):
        piece = lax.reduce_precision(left, 8, 7)
        pieces.append(piece.astype(jnp.bfloat16))
        left = left - piece
    columns = jnp.concatenate(pieces, axis=1)
    return jnp.pad(columns, ((0, 0), (0, -columns.shape[1] % 128)))


def load_kernel(*refs):
    sources, targets, sems = refs[:3], refs[3:6], refs[6]
    copies = [
        pltpu.make_async_copy(source, target, sems.at[place])
        for place, (source, target) in enumerate(zip(sources, targets))
    ]
    for copy in copies:
        copy.start()
    for copy in copies:
        copy.wait()


def load_weights(weights):
    weights = [pltpu.with_memory_space_constraint(value, pltpu.HBM) for value in weights]
    size = sum(2 * value.size for value in weights)
    return pl.pallas_call(
        load_kernel,
        out_shape=[jax.ShapeDtypeStruct(value.shape, value.dtype) for value in weights],
        in_specs=[pl.BlockSpec(memory_space=pltpu.HBM)] * 3,
        out_specs=[pl.BlockSpec(memory_space=pltpu.VMEM)] * 3,
        scratch_shapes=[pltpu.SemaphoreType.DMA((3,))],
        cost_estimate=pl.CostEstimate(flops=0, bytes_accessed=size, transcendentals=0),
        compiler_params=pltpu.CompilerParams(vmem_limit_bytes=2 * 1024 * 1024),
    )(*weights)


def expert_kernel(pieces, expert_count, width, chunk, splits, resident, *refs):
    piece_refs, weight_refs = refs[:pieces], list(refs[pieces : pieces + 6])
    out_refs = refs[pieces + 6 : pieces + 6 + pieces // 2]
    rows, hidden, *loaded = refs[pieces + 6 + pieces // 2 :]
    source_refs = weight_refs[resident:]
    weight_refs[resident:] = loaded[: 6 - resident]
    count = piece_refs[0].shape[0]
    depth = width // splits
    copies = [
        pltpu.make_async_copy(source, target, loaded[-1].at[place])
        for place, (source, target) in enumerate(zip(source_refs, weight_refs[resident:]))
    ]
    for copy in copies:
        copy.start()

    def ready(which):
        if which >= resident:
            copies[which - resident].wait()
        return weight_refs[which]

    expert = lax.div(lax.axis_index("ep"), 2)
    scales = []
    for place, piece_ref in enumerate(piece_refs):
        rows[place * count : (place + 1) * count, :] = piece_ref[:, :width]
        columns = piece_ref[:, width:].astype(jnp.float32)
        lane = lax.broadcasted_iota(jnp.int32, columns.shape, 1)
        mine = (lax.rem(lane, expert_count) == expert) & (lane < 3 * expert_count)
        scales.append(jnp.sum(jnp.where(mine, columns, 0.0), axis=1, keepdims=True))
    for half in range(2):
        totals = []
        for kind in range(2):
            weight_ref, total = ready(3 * half + kind), 0.0
            for part in range(splits):
                inner = slice(part * depth, (part + 1) * depth)
                total += jnp.dot(
                    rows[:, inner], weight_ref[inner, :], preferred_element_type=jnp.float32
                )
            totals.append(total)
        hidden[half] = (jax.nn.silu(totals[0]) * totals[1]).astype(jnp.bfloat16)
        ready(3 * half + 2)
    for start in range(0, width, chunk):
        cols = slice(start, start + chunk)
        value = jnp.dot(hidden[0], weight_refs[2][:, cols], preferred_element_type=jnp.float32)
        value += jnp.dot(hidden[1], weight_refs[5][:, cols], preferred_element_type=jnp.float32)
        for place, scale in enumerate(scales):
            piece = value[place * count : (place + 1) * count] * scale
            target = slice(place % 2 * count, (place % 2 + 1) * count)
            out_refs[place // 2][target, cols] = piece.astype(jnp.bfloat16)


def run_expert(pieces, weights, expert_count):
    count = pieces[0].shape[0]
    units, width = weights[2].shape
    vmem, hbm = pl.BlockSpec(memory_space=pltpu.VMEM), pl.BlockSpec(memory_space=pltpu.HBM)
    rows = count * len(pieces)
    chunk, splits, resident = 512, 2, RESIDENT
    scratch = [
        pltpu.VMEM((rows, width), jnp.bfloat16),
        pltpu.VMEM((2, rows, units), jnp.bfloat16),
    ]
    scratch += [pltpu.VMEM(value.shape, value.dtype) for value in weights[resident:]]
    if resident < 6:
        scratch.append(pltpu.SemaphoreType.DMA((6 - resident,)))
    weights = weights[:resident] + tuple(
        pltpu.with_memory_space_constraint(value, pltpu.HBM) for value in weights[resident:]
    )
    return pl.pallas_call(
        functools.partial(expert_kernel, len(pieces), expert_count, width, chunk, splits, resident),
        out_shape=[jax.ShapeDtypeStruct((2 * count, width), jnp.bfloat16)] * (len(pieces) // 2),
        in_specs=[vmem] * (len(pieces) + resident) + [hbm] * (6 - resident),
        out_specs=[vmem] * (len(pieces) // 2),
        scratch_shapes=scratch,
        cost_estimate=pl.CostEstimate(
            flops=12 * rows * width * units,
            bytes_accessed=12 * width * units + 4 * rows * width,
            transcendentals=2 * rows * units,
        ),
        compiler_params=pltpu.CompilerParams(vmem_limit_bytes=VMEM_MIB * 1024 * 1024),
    )(*pieces, *weights)


def body(tokens, routes, gate_weights, w_gate, w_up, w_down):
    devices = lax.axis_size("ep")
    expert_count = devices // 2
    bits = expert_count.bit_length() - 2
    weights = (w_gate[0], w_up[0], w_down[0])
    swapped = tuple(exchange(value, 1) for value in weights)
    own = load_weights(weights)
    columns = gate_columns(routes, gate_weights, expert_count)
    held = gather_rows(tokens, columns, bits)
    order = sorted(held, key=lambda mask: mask.bit_count())
    pieces = [piece for mask in order for piece in held[mask]]
    sums = run_expert(pieces, tuple(own) + swapped, expert_count)
    return reduce_rows(dict(zip(order, sums)), bits)


def solution(mesh):
    placed = (
        P(("rep", "ep"), None),
        P(("rep", "ep"), None),
        P(("rep", "ep"), None),
        P("ep", None, None),
        P("ep", None, None),
        P("ep", None, None),
    )
    return jax.shard_map(
        body, mesh=mesh, in_specs=placed, out_specs=P(("rep", "ep"), None), check_vma=False
    )
```

```python
import functools

import jax
import jax.numpy as jnp
from jax import lax
from jax.experimental import pallas as pl
from jax.experimental.pallas import tpu as pltpu
from jax.sharding import PartitionSpec as P


RESIDENT, VMEM_MIB = 3, 20


def exchange(value, mask):
    pairs = [(source, source ^ mask) for source in range(lax.axis_size("ep"))]
    return lax.ppermute(value, "ep", pairs)


def tree_plan(bits):
    steps = []
    for hops in range(1, bits):
        chosen = {bit: [] for bit in range(bits)}
        for mask in range(1 << bits):
            if mask.bit_count() == hops:
                held = [bit for bit in range(bits) if mask >> bit & 1]
                bit = min(held, key=lambda candidate: len(chosen[candidate]))
                chosen[bit].append(mask)
        steps.append([(bit, masks) for bit, masks in chosen.items() if masks])
    return steps


def joined(parts):
    return parts[0] if len(parts) == 1 else jnp.concatenate(parts, axis=0)


def gather_tree(own, bits, last_bit):
    count = own.shape[0]
    held = {0: own}
    for step in tree_plan(bits):
        for bit, masks in step:
            sent = joined([held[mask ^ (1 << bit)] for mask in masks])
            arrived = exchange(sent, 2 << bit)
            for place, mask in enumerate(masks):
                held[mask] = arrived[count * place : count * (place + 1)]
    last = (1 << bits) - 1
    held[last] = exchange(held[last ^ (1 << last_bit)], 2 << last_bit)
    return held


def gather_rows(tokens, columns, bits):
    far_tokens = exchange(tokens, 2 << bits)
    far_columns = exchange(columns, 2 << bits)
    near = gather_tree(jnp.concatenate([tokens, columns], axis=1), bits, 0)
    far = gather_tree(jnp.concatenate([far_tokens, far_columns], axis=1), bits, 1)
    return {mask: (near[mask], far[mask]) for mask in near}


def summed(parts):
    if len(parts) == 1:
        return parts[0]
    total = parts[0].astype(jnp.float32)
    for part in parts[1:]:
        total = total + part.astype(jnp.float32)
    return total.astype(parts[0].dtype)


def added(left, right):
    return summed([left, right])


def reduce_rows(held, bits):
    last = (1 << bits) - 1
    count = held[last].shape[0] // 2
    extra = {}
    for bit in range(2):
        rows = slice(bit * count, (bit + 1) * count)
        arrived = exchange(held[last][rows], 2 << bit)
        mask = last ^ (1 << bit)
        halves = [held[mask][:count], held[mask][count:]]
        halves[bit] = added(halves[bit], arrived)
        extra[mask] = jnp.concatenate(halves, axis=0)
    held = {**held, **extra}
    extra = {}
    steps = tree_plan(bits)
    for step in reversed(steps[1:]):
        for bit, masks in step:
            arrived = exchange(joined([held[mask] for mask in masks]), 2 << bit)
            for place, mask in enumerate(masks):
                piece = arrived[2 * count * place : 2 * count * (place + 1)]
                target = mask ^ (1 << bit)
                if target.bit_count() > 1:
                    held[target] = added(held[target], piece)
                else:
                    extra.setdefault(target, []).append(piece)

    def last_sum(rows):
        parts = [held[0][rows]]
        for bit in range(bits):
            sent = [held[1 << bit][rows]] + [piece[rows] for piece in extra.get(1 << bit, [])]
            parts.append(exchange(summed(sent), 2 << bit))
        return parts

    far = summed(last_sum(slice(count, None)))
    arrived = exchange(far, 2 << bits)
    return summed(last_sum(slice(0, count)) + [arrived])


def gate_columns(routes, gate_weights, expert_count):
    hits = routes[:, :, None] == jnp.arange(expert_count, dtype=jnp.int32)[None, None, :]
    left = jnp.sum(jnp.where(hits, gate_weights[:, :, None], 0.0), axis=1)
    pieces = []
    for _ in range(3):
        piece = lax.reduce_precision(left, 8, 7)
        pieces.append(piece.astype(jnp.bfloat16))
        left = left - piece
    columns = jnp.concatenate(pieces, axis=1)
    return jnp.pad(columns, ((0, 0), (0, -columns.shape[1] % 128)))


def load_kernel(*refs):
    sources, targets, sems = refs[:3], refs[3:6], refs[6]
    copies = [
        pltpu.make_async_copy(source, target, sems.at[place])
        for place, (source, target) in enumerate(zip(sources, targets))
    ]
    for copy in copies:
        copy.start()
    for copy in copies:
        copy.wait()


def load_weights(weights):
    weights = [pltpu.with_memory_space_constraint(value, pltpu.HBM) for value in weights]
    size = sum(2 * value.size for value in weights)
    return pl.pallas_call(
        load_kernel,
        out_shape=[jax.ShapeDtypeStruct(value.shape, value.dtype) for value in weights],
        in_specs=[pl.BlockSpec(memory_space=pltpu.HBM)] * 3,
        out_specs=[pl.BlockSpec(memory_space=pltpu.VMEM)] * 3,
        scratch_shapes=[pltpu.SemaphoreType.DMA((3,))],
        cost_estimate=pl.CostEstimate(flops=0, bytes_accessed=size, transcendentals=0),
        compiler_params=pltpu.CompilerParams(vmem_limit_bytes=2 * 1024 * 1024),
    )(*weights)


def expert_kernel(pieces, expert_count, width, chunk, splits, resident, *refs):
    piece_refs, weight_refs = refs[:pieces], list(refs[pieces : pieces + 6])
    out_refs = refs[pieces + 6 : pieces + 6 + pieces // 2]
    rows, hidden, *loaded = refs[pieces + 6 + pieces // 2 :]
    source_refs = weight_refs[resident:]
    weight_refs[resident:] = loaded[: 6 - resident]
    count = piece_refs[0].shape[0]
    depth = width // splits
    copies = [
        pltpu.make_async_copy(source, target, loaded[-1].at[place])
        for place, (source, target) in enumerate(zip(source_refs, weight_refs[resident:]))
    ]
    for copy in copies:
        copy.start()

    def ready(which):
        if which >= resident:
            copies[which - resident].wait()
        return weight_refs[which]

    expert = lax.div(lax.axis_index("ep"), 2)
    scales = []
    for place, piece_ref in enumerate(piece_refs):
        rows[place * count : (place + 1) * count, :] = piece_ref[:, :width]
        columns = piece_ref[:, width:].astype(jnp.float32)
        lane = lax.broadcasted_iota(jnp.int32, columns.shape, 1)
        mine = (lax.rem(lane, expert_count) == expert) & (lane < 3 * expert_count)
        scales.append(jnp.sum(jnp.where(mine, columns, 0.0), axis=1, keepdims=True))
    for half in range(2):
        totals = []
        for kind in range(2):
            weight_ref, total = ready(3 * half + kind), 0.0
            for part in range(splits):
                inner = slice(part * depth, (part + 1) * depth)
                total += jnp.dot(
                    rows[:, inner], weight_ref[inner, :], preferred_element_type=jnp.float32
                )
            totals.append(total)
        hidden[half] = (jax.nn.silu(totals[0]) * totals[1]).astype(jnp.bfloat16)
        ready(3 * half + 2)
    for start in range(0, width, chunk):
        cols = slice(start, start + chunk)
        value = jnp.dot(hidden[0], weight_refs[2][:, cols], preferred_element_type=jnp.float32)
        value += jnp.dot(hidden[1], weight_refs[5][:, cols], preferred_element_type=jnp.float32)
        for place, scale in enumerate(scales):
            piece = value[place * count : (place + 1) * count] * scale
            target = slice(place % 2 * count, (place % 2 + 1) * count)
            out_refs[place // 2][target, cols] = piece.astype(jnp.bfloat16)


def run_expert(pieces, weights, expert_count):
    count = pieces[0].shape[0]
    units, width = weights[2].shape
    vmem, hbm = pl.BlockSpec(memory_space=pltpu.VMEM), pl.BlockSpec(memory_space=pltpu.HBM)
    rows = count * len(pieces)
    chunk, splits, resident = 512, 2, RESIDENT
    scratch = [
        pltpu.VMEM((rows, width), jnp.bfloat16),
        pltpu.VMEM((2, rows, units), jnp.bfloat16),
    ]
    scratch += [pltpu.VMEM(value.shape, value.dtype) for value in weights[resident:]]
    if resident < 6:
        scratch.append(pltpu.SemaphoreType.DMA((6 - resident,)))
    weights = weights[:resident] + tuple(
        pltpu.with_memory_space_constraint(value, pltpu.HBM) for value in weights[resident:]
    )
    return pl.pallas_call(
        functools.partial(expert_kernel, len(pieces), expert_count, width, chunk, splits, resident),
        out_shape=[jax.ShapeDtypeStruct((2 * count, width), jnp.bfloat16)] * (len(pieces) // 2),
        in_specs=[vmem] * (len(pieces) + resident) + [hbm] * (6 - resident),
        out_specs=[vmem] * (len(pieces) // 2),
        scratch_shapes=scratch,
        cost_estimate=pl.CostEstimate(
            flops=12 * rows * width * units,
            bytes_accessed=12 * width * units + 4 * rows * width,
            transcendentals=2 * rows * units,
        ),
        compiler_params=pltpu.CompilerParams(vmem_limit_bytes=VMEM_MIB * 1024 * 1024),
    )(*pieces, *weights)


def body(tokens, routes, gate_weights, w_gate, w_up, w_down):
    devices = lax.axis_size("ep")
    expert_count = devices // 2
    bits = expert_count.bit_length() - 2
    weights = (w_gate[0], w_up[0], w_down[0])
    swapped = tuple(exchange(value, 1) for value in weights)
    own = load_weights(weights)
    columns = gate_columns(routes, gate_weights, expert_count)
    held = gather_rows(tokens, columns, bits)
    order = sorted(held, key=lambda mask: mask.bit_count())
    pieces = [piece for mask in order for piece in held[mask]]
    sums = run_expert(pieces, tuple(own) + swapped, expert_count)
    return reduce_rows(dict(zip(order, sums)), bits)


def solution(mesh):
    placed = (
        P(("rep", "ep"), None),
        P(("rep", "ep"), None),
        P(("rep", "ep"), None),
        P("ep", None, None),
        P("ep", None, None),
        P("ep", None, None),
    )
    return jax.shard_map(
        body, mesh=mesh, in_specs=placed, out_specs=P(("rep", "ep"), None), check_vma=False
    )
```

```python
import functools

import jax
import jax.numpy as jnp
from jax import lax
from jax.experimental import pallas as pl
from jax.experimental.pallas import tpu as pltpu
from jax.sharding import PartitionSpec as P


RESIDENT, VMEM_MIB = 6, 14


def exchange(value, mask):
    pairs = [(source, source ^ mask) for source in range(lax.axis_size("ep"))]
    return lax.ppermute(value, "ep", pairs)


def tree_plan(bits):
    steps = []
    for hops in range(1, bits):
        chosen = {bit: [] for bit in range(bits)}
        for mask in range(1 << bits):
            if mask.bit_count() == hops:
                held = [bit for bit in range(bits) if mask >> bit & 1]
                bit = min(held, key=lambda candidate: len(chosen[candidate]))
                chosen[bit].append(mask)
        steps.append([(bit, masks) for bit, masks in chosen.items() if masks])
    return steps


def joined(parts):
    return parts[0] if len(parts) == 1 else jnp.concatenate(parts, axis=0)


def gather_tree(own, bits, last_bit):
    count = own.shape[0]
    held = {0: own}
    for step in tree_plan(bits):
        for bit, masks in step:
            sent = joined([held[mask ^ (1 << bit)] for mask in masks])
            arrived = exchange(sent, 2 << bit)
            for place, mask in enumerate(masks):
                held[mask] = arrived[count * place : count * (place + 1)]
    last = (1 << bits) - 1
    held[last] = exchange(held[last ^ (1 << last_bit)], 2 << last_bit)
    return held


def gather_rows(tokens, columns, bits):
    far_tokens = exchange(tokens, 2 << bits)
    far_columns = exchange(columns, 2 << bits)
    near = gather_tree(jnp.concatenate([tokens, columns], axis=1), bits, 0)
    far = gather_tree(jnp.concatenate([far_tokens, far_columns], axis=1), bits, 1)
    return {mask: (near[mask], far[mask]) for mask in near}


def summed(parts):
    if len(parts) == 1:
        return parts[0]
    total = parts[0].astype(jnp.float32)
    for part in parts[1:]:
        total = total + part.astype(jnp.float32)
    return total.astype(parts[0].dtype)


def added(left, right):
    return summed([left, right])


def reduce_rows(held, bits):
    last = (1 << bits) - 1
    count = held[last].shape[0] // 2
    extra = {}
    for bit in range(2):
        rows = slice(bit * count, (bit + 1) * count)
        arrived = exchange(held[last][rows], 2 << bit)
        mask = last ^ (1 << bit)
        halves = [held[mask][:count], held[mask][count:]]
        halves[bit] = added(halves[bit], arrived)
        extra[mask] = jnp.concatenate(halves, axis=0)
    held = {**held, **extra}
    extra = {}
    steps = tree_plan(bits)
    for step in reversed(steps[1:]):
        for bit, masks in step:
            arrived = exchange(joined([held[mask] for mask in masks]), 2 << bit)
            for place, mask in enumerate(masks):
                piece = arrived[2 * count * place : 2 * count * (place + 1)]
                target = mask ^ (1 << bit)
                if target.bit_count() > 1:
                    held[target] = added(held[target], piece)
                else:
                    extra.setdefault(target, []).append(piece)

    def last_sum(rows):
        parts = [held[0][rows]]
        for bit in range(bits):
            sent = [held[1 << bit][rows]] + [piece[rows] for piece in extra.get(1 << bit, [])]
            parts.append(exchange(summed(sent), 2 << bit))
        return parts

    far = summed(last_sum(slice(count, None)))
    arrived = exchange(far, 2 << bits)
    return summed(last_sum(slice(0, count)) + [arrived])


def gate_columns(routes, gate_weights, expert_count):
    count = routes.shape[0]
    experts = jnp.arange(expert_count, dtype=jnp.int32)[None, :, None]
    hits = routes.T[:, None, :] == experts
    left = jnp.sum(jnp.where(hits, gate_weights.T[:, None, :], 0.0), axis=0)
    pieces = []
    for _ in range(3):
        piece = lax.reduce_precision(left, 8, 7)
        pieces.append(piece.astype(jnp.bfloat16))
        left = left - piece
    columns = jnp.concatenate(
        [piece[start : start + count] for start in range(0, expert_count, count) for piece in pieces],
        axis=1,
    )
    return jnp.pad(columns, ((0, 0), (0, -columns.shape[1] % 128)))


def load_kernel(*refs):
    sources, targets, sems = refs[:3], refs[3:6], refs[6]
    copies = [
        pltpu.make_async_copy(source, target, sems.at[place])
        for place, (source, target) in enumerate(zip(sources, targets))
    ]
    for copy in copies:
        copy.start()
    for copy in copies:
        copy.wait()


def load_weights(weights):
    weights = [pltpu.with_memory_space_constraint(value, pltpu.HBM) for value in weights]
    size = sum(2 * value.size for value in weights)
    return pl.pallas_call(
        load_kernel,
        out_shape=[jax.ShapeDtypeStruct(value.shape, value.dtype) for value in weights],
        in_specs=[pl.BlockSpec(memory_space=pltpu.HBM)] * 3,
        out_specs=[pl.BlockSpec(memory_space=pltpu.VMEM)] * 3,
        scratch_shapes=[pltpu.SemaphoreType.DMA((3,))],
        cost_estimate=pl.CostEstimate(flops=0, bytes_accessed=size, transcendentals=0),
        compiler_params=pltpu.CompilerParams(vmem_limit_bytes=2 * 1024 * 1024),
    )(*weights)


def expert_kernel(pieces, width, chunk, splits, resident, *refs):
    piece_refs, weight_refs = refs[:pieces], list(refs[pieces : pieces + 6])
    out_refs = refs[pieces + 6 : pieces + 6 + pieces // 2]
    rows, hidden, *loaded = refs[pieces + 6 + pieces // 2 :]
    source_refs = weight_refs[resident:]
    weight_refs[resident:] = loaded[: 6 - resident]
    count = piece_refs[0].shape[0]
    depth = width // splits
    copies = [
        pltpu.make_async_copy(source, target, loaded[-1].at[place])
        for place, (source, target) in enumerate(zip(source_refs, weight_refs[resident:]))
    ]
    for copy in copies:
        copy.start()

    def ready(which):
        if which >= resident:
            copies[which - resident].wait()
        return weight_refs[which]

    expert = lax.div(lax.axis_index("ep"), 2)
    scales = []
    for place, piece_ref in enumerate(piece_refs):
        rows[place * count : (place + 1) * count, :] = piece_ref[:, :width]
        columns = piece_ref[:, width:].astype(jnp.float32)
        row = lax.broadcasted_iota(jnp.int32, columns.shape, 0)
        lane = lax.broadcasted_iota(jnp.int32, columns.shape, 1)
        here = row == lax.rem(expert, count)
        line = jnp.sum(jnp.where(here, columns, 0.0), axis=0, keepdims=True)
        mine = (lax.rem(lane, count) == row) & (lax.div(lane, 3 * count) == lax.div(expert, count))
        scales.append(jnp.sum(jnp.where(mine, line, 0.0), axis=1, keepdims=True))
    for half in range(2):
        totals = []
        for kind in range(2):
            weight_ref, total = ready(3 * half + kind), 0.0
            for part in range(splits):
                inner = slice(part * depth, (part + 1) * depth)
                total += jnp.dot(
                    rows[:, inner], weight_ref[inner, :], preferred_element_type=jnp.float32
                )
            totals.append(total)
        hidden[half] = (jax.nn.silu(totals[0]) * totals[1]).astype(jnp.bfloat16)
        ready(3 * half + 2)
    for start in range(0, width, chunk):
        cols = slice(start, start + chunk)
        value = jnp.dot(hidden[0], weight_refs[2][:, cols], preferred_element_type=jnp.float32)
        value += jnp.dot(hidden[1], weight_refs[5][:, cols], preferred_element_type=jnp.float32)
        for place, scale in enumerate(scales):
            piece = value[place * count : (place + 1) * count] * scale
            target = slice(place % 2 * count, (place % 2 + 1) * count)
            out_refs[place // 2][target, cols] = piece.astype(jnp.bfloat16)


def run_expert(pieces, weights):
    count = pieces[0].shape[0]
    units, width = weights[2].shape
    vmem, hbm = pl.BlockSpec(memory_space=pltpu.VMEM), pl.BlockSpec(memory_space=pltpu.HBM)
    rows = count * len(pieces)
    chunk, splits, resident = 512, 2, RESIDENT
    scratch = [
        pltpu.VMEM((rows, width), jnp.bfloat16),
        pltpu.VMEM((2, rows, units), jnp.bfloat16),
    ]
    scratch += [pltpu.VMEM(value.shape, value.dtype) for value in weights[resident:]]
    if resident < 6:
        scratch.append(pltpu.SemaphoreType.DMA((6 - resident,)))
    weights = weights[:resident] + tuple(
        pltpu.with_memory_space_constraint(value, pltpu.HBM) for value in weights[resident:]
    )
    return pl.pallas_call(
        functools.partial(expert_kernel, len(pieces), width, chunk, splits, resident),
        out_shape=[jax.ShapeDtypeStruct((2 * count, width), jnp.bfloat16)] * (len(pieces) // 2),
        in_specs=[vmem] * (len(pieces) + resident) + [hbm] * (6 - resident),
        out_specs=[vmem] * (len(pieces) // 2),
        scratch_shapes=scratch,
        cost_estimate=pl.CostEstimate(
            flops=12 * rows * width * units,
            bytes_accessed=12 * width * units + 4 * rows * width,
            transcendentals=2 * rows * units,
        ),
        compiler_params=pltpu.CompilerParams(vmem_limit_bytes=VMEM_MIB * 1024 * 1024),
    )(*pieces, *weights)


def body(tokens, routes, gate_weights, w_gate, w_up, w_down):
    devices = lax.axis_size("ep")
    expert_count = devices // 2
    bits = expert_count.bit_length() - 2
    weights = (w_gate[0], w_up[0], w_down[0])
    swapped = tuple(exchange(value, 1) for value in weights)
    own = load_weights(weights)
    columns = gate_columns(routes, gate_weights, expert_count)
    held = gather_rows(tokens, columns, bits)
    order = sorted(held, key=lambda mask: mask.bit_count())
    pieces = [piece for mask in order for piece in held[mask]]
    sums = run_expert(pieces, tuple(own) + swapped)
    return reduce_rows(dict(zip(order, sums)), bits)


def solution(mesh):
    placed = (
        P(("rep", "ep"), None),
        P(("rep", "ep"), None),
        P(("rep", "ep"), None),
        P("ep", None, None),
        P("ep", None, None),
        P("ep", None, None),
    )
    return jax.shard_map(
        body, mesh=mesh, in_specs=placed, out_specs=P(("rep", "ep"), None), check_vma=False
    )
```
